256 devices in a mesh: seq: 64 (over y_hi, z, x), fsdp: 4 (over y_lo, core).
Axes of the slice: x: 4, y: 4 (y_hi: 2, y_lo: 2; y = y_hi * 2 + y_lo), z: 8, core: 2. Of those that a mesh axis runs over, the one named last changes fastest.
Arguments:
- image_query: bfloat16 [4, 16384, 1536], P('fsdp', 'seq'), may hold values from -6 to 6
- image_key: bfloat16 [4, 16384, 1536], P('fsdp', 'seq'), may hold values from -6 to 6
- image_value: bfloat16 [4, 16384, 1536], P('fsdp', 'seq'), may hold values from -6 to 6
- text_key: bfloat16 [4, 512, 1536], P('fsdp'), may hold values from -6 to 6
- text_value: bfloat16 [4, 512, 1536], P('fsdp'), may hold values from -6 to 6
- out_weight: bfloat16 [1536, 1536], P('fsdp'), may hold values from -0.15625 to 0.15625
- cotangent: bfloat16 [4, 16384, 1536], P('fsdp', 'seq'), may hold values from -16 to 16
Outputs:
- image_out: bfloat16 [4, 16384, 1536], P('fsdp', 'seq')
- grad_query: bfloat16 [4, 16384, 1536], P('fsdp', 'seq')
- grad_key: bfloat16 [4, 16384, 1536], P('fsdp', 'seq')
- grad_value: bfloat16 [4, 16384, 1536], P('fsdp', 'seq')
- grad_weight: float32 [1536, 1536], P(('fsdp', 'seq'))
The draws below stay inside these ranges and needn't reach their ends.
All inputs are finite; a program needn't handle non-finite values.
Results may differ from the reference program's by a relative error of at most 0.0095.
Values may be sent and summed in bfloat16 or wider, within the bound.
A program may use at most 128 MiB of HBM per device.

```python
import math
import jax
import jax.numpy as jnp
from jax import lax

HEAD_DIM = 128
OUT_WIDTH = 1536
TEXT = 512
STEPS = 4
TOK_DEV = 256
INNER = 1536
IMAGE = 16384
SAMPLES = 4
N_SEQ = 64


def draw_image_query(key, part):
    shape = (SAMPLES, IMAGE, INNER)
    base = jnp.clip(jax.random.normal(jax.random.fold_in(key, 11), shape, jnp.float32), -5.0, 5.0)
    return base.astype(jnp.bfloat16)


def draw_image_key(key, part):
    shape = (SAMPLES, IMAGE, INNER)
    base = jnp.clip(jax.random.normal(jax.random.fold_in(key, 21), shape, jnp.float32), -5.0, 5.0)
    return base.astype(jnp.bfloat16)


def spiked(entries, key, source, target, parts, factor):
    def block_of(axis_at):
        return (jnp.arange(entries.shape[axis_at]) // (entries.shape[axis_at] // parts)).reshape((-1,) + (1,) * (entries.ndim - 1 - axis_at))

    first = jax.random.permutation(key, parts)[block_of(target)]
    far = (block_of(target) + parts // 2) % parts
    return jnp.where((block_of(source) == first) | (block_of(source) == far), factor * entries, entries)


def shard_levels(rng, shape, pieces, smallest, high):
    def one(dim, parts):
        steps = jax.random.uniform(jax.random.fold_in(jax.random.fold_in(rng, 6), dim), (parts,), jnp.float32, smallest / len(pieces), high / len(pieces))
        return jnp.repeat(jnp.exp(steps), shape[dim] // parts).reshape((-1,) + (1,) * (len(shape) - dim - 1))

    gain = one(*pieces[0])
    for cut in pieces[1:]:
        gain = gain * one(*cut)
    return gain


def centred(stream_key, dims, spread, reach, cuts=(), held_as=jnp.bfloat16):
    gain = shard_levels(stream_key, dims, cuts, -0.22, 0.18) if cuts else 1.0
    entries = jax.random.normal(stream_key, dims, jnp.float32) * spread * gain
    return jnp.minimum(jnp.maximum(entries, -reach), reach).astype(held_as)


def gaussian_with(key, extent, spread, bound, pieces, heavy, held_as=jnp.bfloat16):
    drawn = spread * jax.random.normal(key, extent, jnp.float32)
    if pieces:
        drawn = drawn * shard_levels(key, extent, pieces, -0.22, 0.18)
    return jnp.clip(spiked(drawn, jax.random.fold_in(key, 3), *heavy), -bound, bound).astype(held_as)


def setup_inputs(seed: int = 0) -> dict:
    streams_of = jax.random.split(jax.random.key(seed), 8)
    return {
        "image_query": draw_image_query(jax.random.fold_in(streams_of[7], 71), 0),
        "image_key": draw_image_key(jax.random.fold_in(streams_of[7], 71), 0),
        "image_value": centred(streams_of[2], (SAMPLES, IMAGE, INNER), 1.0, 6.0, ((0, 4), (1, 64))),
        "text_key": centred(streams_of[3], (SAMPLES, TEXT, INNER), 1.0, 6.0, ((0, 4),)),
        "text_value": centred(streams_of[4], (SAMPLES, TEXT, INNER), 1.0, 6.0, ((0, 4),)),
        "out_weight": centred(streams_of[5], (INNER, OUT_WIDTH), INNER ** -0.5, 0.15625, ((0, 4),)),
        "cotangent": gaussian_with(streams_of[6], (SAMPLES, IMAGE, OUT_WIDTH), 1.0, 16.0, ((0, 4), (1, 64)), (1, 2, 64, 4.0)),
    }


def head_pass(inputs):
    head_query, head_key, head_value, head_grad = inputs
    scaling = 1.0 / math.sqrt(head_query.shape[1])
    scores = lax.dot_general(head_query, head_key, (((1,), (1,)), ((), ())), preferred_element_type=jnp.float32) * scaling
    row_peak = lax.optimization_barrier(jnp.max(scores, axis=1, keepdims=True))
    shifted = jnp.exp(scores - row_peak)
    softmax = shifted / lax.optimization_barrier(jnp.sum(shifted, axis=1, keepdims=True))
    prob_low = softmax.astype(jnp.bfloat16)
    attended = jnp.dot(prob_low, head_value, preferred_element_type=jnp.float32).astype(jnp.bfloat16)
    row_delta = lax.optimization_barrier(jnp.sum(head_grad.astype(jnp.float32) * attended.astype(jnp.float32), axis=1, keepdims=True))
    grad_prob = lax.dot_general(head_grad, head_value, (((1,), (1,)), ((), ())), preferred_element_type=jnp.float32)
    grad_score = (softmax * (grad_prob - row_delta) * scaling).astype(jnp.bfloat16)
    grad_q = jnp.dot(grad_score, head_key, preferred_element_type=jnp.float32).astype(jnp.bfloat16)
    grad_k = lax.dot_general(grad_score, head_query, (((0,), (0,)), ((), ())), preferred_element_type=jnp.float32)
    grad_v = lax.dot_general(prob_low, head_grad, (((0,), (0,)), ((), ())), preferred_element_type=jnp.float32)
    return (attended, grad_q, grad_k, grad_v)

def split_heads(matrix, width):
    return matrix.reshape(matrix.shape[0], -1, width).transpose(1, 0, 2)

def merge_heads(stacked):
    return stacked.transpose(1, 0, 2).reshape(stacked.shape[1], -1)

def reference(image_query, image_key, image_value, text_key, text_value, out_weight, cotangent):
    out_list, query_list, key_list, value_list = ([], [], [], [])
    grad_weight = jnp.zeros((INNER, OUT_WIDTH), jnp.float32)
    for sample in range(SAMPLES):
        queries = image_query[sample]
        keys_all = image_key[sample]
        values_all = image_value[sample]
        grad_attended = lax.dot_general(cotangent[sample], out_weight, (((1,), (1,)), ((), ())), preferred_element_type=jnp.float32).astype(jnp.bfloat16)

        def visit_block(running, block_index):
            key_sum, value_sum = running
            window = ((block_index - STEPS + 1) * TOK_DEV + jnp.arange(STEPS * TOK_DEV, dtype=jnp.int32)) % IMAGE
            window = window.astype(jnp.int32)
            first_row = (block_index * TOK_DEV).astype(jnp.int32)
            block_query = lax.dynamic_slice_in_dim(queries, first_row, TOK_DEV, 0)
            block_grad = lax.dynamic_slice_in_dim(grad_attended, first_row, TOK_DEV, 0)
            set_keys = jnp.concatenate([text_key[sample], jnp.take(keys_all, window, axis=0)], axis=0)
            set_values = jnp.concatenate([text_value[sample], jnp.take(values_all, window, axis=0)], axis=0)
            attended, grad_q, grad_k, grad_v = lax.map(head_pass, (split_heads(block_query, HEAD_DIM), split_heads(set_keys, HEAD_DIM), split_heads(set_values, HEAD_DIM), split_heads(block_grad, HEAD_DIM)))
            key_sum = key_sum.at[window].add(merge_heads(grad_k)[TEXT:])
            value_sum = value_sum.at[window].add(merge_heads(grad_v)[TEXT:])
            return ((key_sum, value_sum), (merge_heads(attended), merge_heads(grad_q)))
        empty_sum = jnp.zeros((IMAGE, INNER), jnp.float32)
        (key_sum, value_sum), (attended, grad_q) = lax.scan(visit_block, (empty_sum, empty_sum), jnp.arange(N_SEQ, dtype=jnp.int32))
        attended = attended.reshape(IMAGE, INNER)
        grad_q = grad_q.reshape(IMAGE, INNER)
        out_list.append(jnp.dot(attended, out_weight, preferred_element_type=jnp.float32).astype(jnp.bfloat16))
        grad_weight = grad_weight + lax.dot_general(attended, cotangent[sample], (((0,), (0,)), ((), ())), preferred_element_type=jnp.float32)
        query_list.append(grad_q)
        key_list.append(key_sum.astype(jnp.bfloat16))
        value_list.append(value_sum.astype(jnp.bfloat16))
    return (jnp.stack(out_list), jnp.stack(query_list), jnp.stack(key_list), jnp.stack(value_list), grad_weight)
```

```python
import functools
import math

import jax
import jax.numpy as jnp
from jax import lax
from jax.experimental import pallas as pl
from jax.experimental.pallas import tpu as pltpu
from jax.sharding import PartitionSpec as P

F32 = jnp.float32
BF16 = jnp.bfloat16
MESH = pl.DeviceIdType.MESH
HEAD = 128
TOK = 256
TEXT = 512
INNER = 1536
SCALE = 1.0 / math.sqrt(HEAD)
COEF = SCALE * math.log2(math.e)
HALO = 3 * TOK
OWN = TEXT + HALO
KEYS = OWN + 4 * TOK
SHARD = 384


def dot(a, b, ca, cb):
    return lax.dot_general(a, b, (((ca,), (cb,)), ((), ())), preferred_element_type=F32)


def rows_at(start, size):
    return pl.ds(pl.multiple_of(start, size), size)


def forward_unit(query, key_at, value_at, prob_ref, score_ref):
    peak = None
    for i in range(6):
        score = dot(key_at(i), query, 1, 1)
        score_ref[i] = score
        part = jnp.max(score, axis=0, keepdims=True)
        peak = part if peak is None else jnp.maximum(peak, part)
    peak = peak * COEF
    total = None
    attended = None
    for i in range(6):
        prob = jnp.exp2(score_ref[i] * COEF - peak)
        part = jnp.sum(prob, axis=0, keepdims=True)
        total = part if total is None else total + part
        low = prob.astype(BF16)
        prob_ref[i] = low
        term = dot(value_at(i), low, 0, 0)
        attended = term if attended is None else attended + term
    inverse = 1.0 / total
    return (attended * inverse).T.astype(BF16), inverse


def backward_unit(query, grad, attended, inverse, key_at, value_at, prob_ref, add_key, add_value):
    grad32 = grad.astype(F32)
    delta = jnp.sum((grad32 * attended.astype(F32)).T, axis=0, keepdims=True)
    query_t = (query.astype(F32).T * (inverse * SCALE)).astype(BF16)
    grad_t = (grad32.T * inverse).astype(BF16)
    total = None
    for i in range(6):
        grad_prob = dot(value_at(i), grad, 1, 1)
        low = prob_ref[i]
        grad_score = (low.astype(F32) * (grad_prob - delta)).astype(BF16)
        term = dot(key_at(i), grad_score, 0, 0)
        total = term if total is None else total + term
        if i >= 2:
            add_key(i - 2, dot(grad_score, query_t, 1, 1))
            add_value(i - 2, dot(low, grad_t, 1, 1))
    return (total * (inverse * SCALE)).T.astype(BF16)


def device(x, y, z, core):
    return ((y // 2) * 32 + z * 4 + x, (y % 2) * 2 + core)


def kernel(
    q_hbm, k_hbm, v_hbm, tk_hbm, tv_hbm, w_hbm, cot_hbm,
    img_hbm, dq_hbm, dk_hbm, dv_hbm, gw_ref,
    img, cot, wf, kb, vb, qb, gs, gb, prob, score, stat, ob, dqb, att,
    dka, dva, hsk, hsv, hrk, hrv, okb, ovb,
    relf, relb, gacc, gsend, grecv, ysend, yrecv, gsum, hsend, hrecv, yown, zsend, zrecv, xsend, xrecv,
    lsem, s_in, r_in, s_gr, r_gr, s_w, r_w, s_halo, r_halo,
    r_rf, s_rf, r_rb, s_rb, s_att, r_att, s_dq, r_dq, s_dkv, r_dkv, s_hb, r_hb,
    s_c, r_c, s_y, r_y, s_h, r_h, s_z, r_z, s_x, r_x,
):
    seq = lax.axis_index("seq")
    fsdp = lax.axis_index("fsdp")
    x = lax.rem(seq, 4)
    z = lax.rem(seq // 4, 8)
    yh = seq // 32
    yl = fsdp // 2
    y = yh * 2 + yl
    core = lax.rem(fsdp, 2)
    zz = yh * 8 + z

    def x_peer(d):
        return device(lax.rem(x + d, 4), y, z, core)

    def y_peer(d):
        return device(x, lax.rem(y + d, 4), z, core)

    def z_peer(d):
        return device(x, y, lax.rem(z + d, 8), core)

    def other_core():
        return device(x, y, z, 1 - core)

    def super_peer(d):
        there = lax.rem(zz + d, 16)
        return device(x, (there // 8) * 2 + yl, lax.rem(there, 8), core)

    def remote(src, dst, ssem, rsem, dev):
        return pltpu.make_async_remote_copy(
            src_ref=src, dst_ref=dst, send_sem=ssem, recv_sem=rsem,
            device_id=dev, device_id_type=MESH,
        )

    pending = []

    def send(*args):
        copy = remote(*args)
        copy.start()
        pending.append(copy)

    def got(dst, ssem, rsem):
        remote(dst, dst, ssem, rsem, other_core()).wait_recv()

    barrier = pltpu.get_barrier_semaphore()
    peers = [x_peer(d) for d in (1, 2, 3)] + [y_peer(d) for d in (1, 2, 3)]
    peers += [z_peer(d) for d in range(1, 8)] + [other_core(), super_peer(1), super_peer(15)]
    for peer in peers:
        pl.semaphore_signal(barrier, inc=1, device_id=peer, device_id_type=MESH)

    locals_ = {}
    count = [0]

    def local(name, src, dst):
        copy = pltpu.make_async_copy(src, dst, lsem.at[count[0]])
        count[0] += 1
        copy.start()
        locals_[name] = copy

    def head(owner, c):
        return rows_at((owner * 3 + c) * HEAD, HEAD)

    own_rows = rows_at(OWN + x * TOK, TOK)
    q_rows = rows_at(x * TOK, TOK)
    local("cot", cot_hbm, cot)
    local("w", w_hbm, wf.at[rows_at(fsdp * SHARD, SHARD)])
    for c in range(3):
        local(("k", c), k_hbm.at[:, head(x, c)], kb.at[c, own_rows])
        local(("v", c), v_hbm.at[:, head(x, c)], vb.at[c, own_rows])
        local(("q", c), q_hbm.at[:, head(x, c)], qb.at[c, q_rows])
        local(("tk", c), tk_hbm.at[:, head(x, c)], kb.at[c, 0:TEXT])
        local(("tv", c), tv_hbm.at[:, head(x, c)], vb.at[c, 0:TEXT])
    for c in range(3):
        dka[c] = jnp.zeros((7 * TOK, HEAD), F32)
        dva[c] = jnp.zeros((7 * TOK, HEAD), F32)
    pl.semaphore_wait(barrier, len(peers))

    half = SHARD // 2
    for d, part in ((1, 0), (3, 1)):
        send(w_hbm.at[part * half:(part + 1) * half], wf.at[rows_at(fsdp * SHARD + part * half, half)],
             s_w.at[part], r_w.at[part], y_peer(d))
    send(w_hbm, wf.at[rows_at(fsdp * SHARD, SHARD)], s_w.at[2], r_w.at[2], other_core())

    for c in range(3):
        for t, (src, dst, at) in enumerate(((k_hbm, kb, own_rows), (v_hbm, vb, own_rows), (q_hbm, qb, q_rows))):
            for d in (1, 3, 2):
                send(src.at[:, head(lax.rem(x + d, 4), c)], dst.at[c, at],
                     s_in.at[t, c, d - 1], r_in.at[t, c, d - 1], x_peer(d))
    def got_in(t, c):
        dst, base = ((kb, OWN), (vb, OWN), (qb, 0))[t]
        for d in (1, 2, 3):
            got(dst.at[c, rows_at(base + lax.rem(x + 4 - d, 4) * TOK, TOK)],
                s_in.at[t, c, d - 1], r_in.at[t, c, d - 1])
        locals_[("k", c) if t == 0 else ("v", c) if t == 1 else ("q", c)].wait()

    def grad_shard(i, owner):
        value = dot(cot[...], wf[rows_at(owner * SHARD, SHARD), :], 1, 1).astype(BF16)
        gs[i] = value
        d = lax.rem(owner + 4 - x, 4)
        copy = remote(gs.at[i], gb.at[q_rows], s_gr.at[i], r_gr.at[d], device(owner, y, z, core))

        @pl.when(d == 0)
        def _():
            gb[q_rows, :] = value

        @pl.when(d != 0)
        def _():
            copy.start()

        return d, copy

    def halo_send(c, t):
        got_in(t, c)
        buf = (kb, vb)[t]
        src = buf.at[c, OWN + TOK:KEYS]
        copy = remote(src, buf.at[c, TEXT:OWN], s_halo.at[t, c], r_halo.at[t, c], super_peer(1))
        pending.append(copy)
        if t == 1 or c == 0:
            copy.start()
            return

        @pl.when(z != 7)
        def _():
            copy.start()

        @pl.when(z == 7)
        def _():
            remote(src, relf.at[c], s_halo.at[t, c], r_rf.at[c], y_peer(2)).start()

    def relay_f(c):
        @pl.when(z == 7)
        def _():
            got(relf.at[c], s_rf.at[c], r_rf.at[c])
            remote(relf.at[c], kb.at[c, TEXT:OWN], s_rf.at[c], r_halo.at[0, c], z_peer(1)).start()

    def relay_b(c):
        @pl.when(z == 0)
        def _():
            got(relb.at[c], s_rb.at[c], r_rb.at[c])
            remote(relb.at[c], hrk.at[c], s_rb.at[c], r_hb.at[0, c], z_peer(7)).start()

    def halo_got(c):
        for t, buf in enumerate((kb, vb)):
            got(buf.at[c, TEXT:OWN], s_halo.at[t, c], r_halo.at[t, c])

    own_f = yl * 2 + core
    core_f = yl * 2 + 1 - core
    y_f = (1 - yl) * 2 + core
    diag_f = (1 - yl) * 2 + 1 - core
    locals_["cot"].wait()
    locals_["w"].wait()
    grads = [grad_shard(0, own_f)]
    halo_send(0, 0)
    got(wf.at[rows_at(core_f * SHARD, SHARD)], s_w.at[2], r_w.at[2])
    grads.append(grad_shard(1, core_f))
    halo_send(0, 1)
    relay = remote(wf.at[rows_at(y_f * SHARD, SHARD)], wf.at[rows_at(y_f * SHARD, SHARD)], s_w.at[3], r_w.at[3], other_core())

    def weight_y():
        for part in (0, 1):
            got(wf.at[rows_at(y_f * SHARD + part * half, half)], s_w.at[part], r_w.at[part])
        relay.start()
        return grad_shard(2, y_f)

    def weight_diag():
        got(wf.at[rows_at(diag_f * SHARD, SHARD)], s_w.at[3], r_w.at[3])
        return grad_shard(3, diag_f)

    @pl.when(z != 0)
    def _():
        weight_y()

    halo_send(1, 0)
    halo_send(1, 1)

    @pl.when(z != 0)
    def _():
        weight_diag()

    def chunk_at(ref, c, b):
        def at(i):
            if i < 2:
                return ref[c, i * TOK:(i + 1) * TOK, :]
            return ref[c, rows_at(TEXT + (b + i - 2) * TOK, TOK), :]
        return at

    def back_copy(src, dst, ssem, rsem, c, b):
        d = lax.rem(b + 4 - x, 4)
        return remote(src, dst.at[:, head(x, c)], ssem.at[c, b], rsem.at[c, d], device(b, y, z, core))

    def forward(c, j):
        b = 3 - j
        rows = rows_at(b * TOK, TOK)
        out, inverse = forward_unit(qb[c, rows, :], chunk_at(kb, c, b), chunk_at(vb, c, b), prob.at[c * 4 + b], score)
        stat[c * 4 + b, 0:1, :] = inverse
        ob[c, rows, :] = out

        @pl.when(b == x)
        def _():
            att[:, head(x, c)] = out

        @pl.when(b != x)
        def _():
            back_copy(ob.at[c, rows], att, s_att, r_att, c, b).start()

    def backward(c, j):
        b = 3 - j
        rows = rows_at(b * TOK, TOK)

        def adder(ref):
            def add(i, value):
                at = rows_at((b + i) * TOK, TOK)
                ref[c, at, :] += value
            return add

        out = backward_unit(
            qb[c, rows, :], gb[rows, c * HEAD:(c + 1) * HEAD], ob[c, rows, :], stat[c * 4 + b, 0:1, :],
            chunk_at(kb, c, b), chunk_at(vb, c, b), prob.at[c * 4 + b], adder(dka), adder(dva))
        dqb[c, rows, :] = out

        @pl.when(b != x)
        def _():
            back_copy(dqb.at[c, rows], dq_hbm, s_dq, r_dq, c, b).start()

    def loop(fn, c, start, stop):
        def body(j, carry):
            fn(c, j)
            return carry
        lax.fori_loop(start, stop, body, 0)

    def finish(c):
        for t, (acc, recv, out, dst) in enumerate(((dka, hrk, okb, dk_hbm), (dva, hrv, ovb, dv_hbm))):
            got(recv.at[c], s_hb.at[t, c], r_hb.at[t, c])
            out[c, 0:TOK, :] = acc[c, HALO:HALO + TOK, :].astype(BF16)
            out[c, TOK:4 * TOK, :] = (acc[c, HALO + TOK:HALO + 4 * TOK, :] + recv[c].astype(F32)).astype(BF16)
            for d in (1, 3, 2):
                b = lax.rem(x + d, 4)
                send(out.at[c, rows_at(b * TOK, TOK)], dst.at[:, head(x, c)],
                     s_dkv.at[t, c, d - 1], r_dkv.at[t, c, d - 1], x_peer(d))
            local(("out", t, c), out.at[c, q_rows], dst.at[:, head(x, c)])

    def project(c):
        for d in (1, 2, 3):
            got(att.at[:, head(lax.rem(x + 4 - d, 4), c)], s_att.at[c, 0], r_att.at[c, d])
        for i in range(2):
            gsend[c, i] = dot(att[:, head(i * 2 + 1 - core, c)], cot[...], 0, 0).astype(BF16)
        send(gsend.at[c], grecv.at[c], s_c.at[c], r_c.at[c], other_core())
        for i in range(2):
            gacc[c, i] = dot(att[:, head(i * 2 + core, c)], cot[...], 0, 0)

    def y_phase(c):
        got(grecv.at[c], s_c.at[c], r_c.at[c])
        ysend[c] = (gacc[c, 1 - yl] + grecv[c, 1 - yl].astype(F32)).astype(BF16)
        for i, d in enumerate((1, 3)):
            at = slice(i * 64, (i + 1) * 64)
            send(ysend.at[c, at], yrecv.at[c, at], s_y.at[c, i], r_y.at[c, i], y_peer(d))
        gsum[c * HEAD:(c + 1) * HEAD, :] = gacc[c, yl] + grecv[c, yl].astype(F32)

    def y_merge(c):
        for i in range(2):
            got(yrecv.at[c, i * 64:(i + 1) * 64], s_y.at[c, i], r_y.at[c, i])
        gsum[c * HEAD:(c + 1) * HEAD, :] += yrecv[c].astype(F32)

    def h_copy(h):
        return remote(hsend.at[h], hrecv.at[h], s_h.at[h], r_h.at[h], y_peer(2))

    def h_phase():
        for h in range(2):
            hsend[h] = gsum[rows_at((1 - yh) * 192 + h * 96, 96), :].astype(BF16)
            h_copy(h).start()

    def z_copy(t):
        d = lax.rem(t + 8 - z, 8)
        return remote(zsend.at[t], zrecv.at[d], s_z.at[t], r_z.at[d], device(x, y, t, core))

    def z_phase(h):
        got(hrecv.at[h], s_h.at[h], r_h.at[h])
        yown[h * 96:(h + 1) * 96, :] = gsum[rows_at(yh * 192 + h * 96, 96), :] + hrecv[h].astype(F32)
        for t in range(4 * h, 4 * h + 4):
            zsend[t] = yown[t * 24:(t + 1) * 24, :].astype(BF16)

            @pl.when(z != t)
            def _(t=t):
                z_copy(t).start()

    def x_phase():
        total = yown[pl.ds(pl.multiple_of(z * 24, 8), 24), :]
        for d in range(1, 8):
            got(zrecv.at[d], s_z.at[d], r_z.at[d])
            total = total + zrecv[d].astype(F32)
        for i in range(4):
            xsend[i] = total[i * 6:(i + 1) * 6]
        for d in (2, 1, 3):
            send(xsend.at[lax.rem(x + d, 4)], xrecv.at[d - 1], s_x.at[d - 1], r_x.at[d - 1], x_peer(d))

    def x_done():
        total = xsend[x]
        for d in range(1, 4):
            got(xrecv.at[d - 1], s_x.at[d - 1], r_x.at[d - 1])
            total = total + xrecv[d - 1]
        gw_ref[...] = total

    def image():
        for n in range(3):
            at = slice(n * 512, (n + 1) * 512)
            img[:, at] = dot(att[...], wf[:, at], 1, 0).astype(BF16)
        local("img", img, img_hbm)

    def forward_chunk(c):
        got_in(2, c)
        locals_[("tk", c)].wait()
        locals_[("tv", c)].wait()
        halo_got(c)
        loop(forward, c, 0, 4)

    def backward_end(c):
        local(("dq", c), dqb.at[c, q_rows], dq_hbm.at[:, head(x, c)])
        for t, (acc, out, recv) in enumerate(((dka, hsk, hrk), (dva, hsv, hrv))):
            out[c] = acc[c, 0:HALO, :].astype(BF16)
            copy = remote(out.at[c], recv.at[c], s_hb.at[t, c], r_hb.at[t, c], super_peer(15))
            pending.append(copy)
            if t == 1:
                copy.start()
                continue

            @pl.when(z != 0)
            def _(copy=copy):
                copy.start()

            @pl.when(z == 0)
            def _(out=out, t=t):
                remote(out.at[c], relb.at[c], s_hb.at[t, c], r_rb.at[c], y_peer(2)).start()

    forward_chunk(0)
    halo_send(2, 0)
    relay_f(1)
    halo_send(2, 1)

    @pl.when(z == 0)
    def _():
        weight_y()

    forward_chunk(1)
    relay_f(2)

    @pl.when(z == 0)
    def _():
        weight_diag()

    forward_chunk(2)
    for i, owner in ((2, y_f), (3, diag_f)):
        d = lax.rem(owner + 4 - x, 4)
        grads.append((d, remote(gs.at[i], gb.at[q_rows], s_gr.at[i], r_gr.at[d], device(owner, y, z, core))))
    pending.append(relay)
    for d in (1, 2, 3):
        got(gb.at[rows_at(lax.rem(x + 4 - d, 4) * TOK, TOK)], s_gr.at[0], r_gr.at[d])
    loop(backward, 0, 0, 2)
    project(0)
    loop(backward, 0, 2, 4)
    backward_end(0)
    project(1)
    y_phase(0)
    project(2)
    loop(backward, 1, 0, 1)
    y_phase(1)
    loop(backward, 1, 1, 2)
    y_phase(2)
    loop(backward, 1, 2, 4)
    backward_end(1)
    relay_b(0)
    loop(backward, 2, 0, 2)

    def merge():
        for c in range(3):
            y_merge(c)
        h_phase()

    @pl.when(z != 0)
    def _():
        merge()

    loop(backward, 2, 2, 4)
    backward_end(2)
    relay_b(1)

    @pl.when(z == 0)
    def _():
        merge()

    for h in range(2):
        pending.append(h_copy(h))
    finish(0)
    image()
    relay_b(2)
    finish(1)
    z_phase(0)
    z_phase(1)
    finish(2)
    x_phase()
    for c in range(3):
        for d in (1, 2, 3):
            cols = head(lax.rem(x + 4 - d, 4), c)
            got(dq_hbm.at[:, cols], s_dq.at[c, 0], r_dq.at[c, d])
            got(dk_hbm.at[:, cols], s_dkv.at[0, c, d - 1], r_dkv.at[0, c, d - 1])
            got(dv_hbm.at[:, cols], s_dkv.at[1, c, d - 1], r_dkv.at[1, c, d - 1])
    x_done()

    for copy in pending:
        copy.wait_send()
    for d, copy in grads:
        @pl.when(d != 0)
        def _(copy=copy):
            copy.wait_send()
    for t in range(8):
        @pl.when(z != t)
        def _(t=t):
            z_copy(t).wait_send()
    for c in (1, 2):
        @pl.when(z == 7)
        def _(c=c):
            remote(relf.at[c], kb.at[c, TEXT:OWN], s_rf.at[c], r_halo.at[0, c], z_peer(1)).wait_send()

    for c in range(3):
        @pl.when(z == 0)
        def _(c=c):
            remote(relb.at[c], hrk.at[c], s_rb.at[c], r_hb.at[0, c], z_peer(7)).wait_send()
    locals_["img"].wait()
    for c in range(3):
        locals_[("dq", c)].wait()
        for t in range(2):
            locals_[("out", t, c)].wait()
        for b in range(4):
            @pl.when(b != x)
            def _(c=c, b=b):
                rows = pl.ds(b * TOK, TOK)
                back_copy(ob.at[c, rows], att, s_att, r_att, c, b).wait_send()
                back_copy(dqb.at[c, rows], dq_hbm, s_dq, r_dq, c, b).wait_send()


def per_device(image_query, image_key, image_value, text_key, text_value, out_weight, cotangent):
    any_ = pl.BlockSpec(memory_space=pl.ANY)
    vmem = pl.BlockSpec(memory_space=pltpu.VMEM)
    dma = pltpu.SemaphoreType.DMA
    block = jax.ShapeDtypeStruct((TOK, INNER), BF16)
    V = pltpu.VMEM
    img, dq, dk, dv, gw = pl.pallas_call(
        kernel,
        out_shape=(block, block, block, block, jax.ShapeDtypeStruct((6, INNER), F32)),
        in_specs=[any_] * 7,
        out_specs=(any_, any_, any_, any_, vmem),
        scratch_shapes=[
            V((TOK, INNER), BF16), V((TOK, INNER), BF16), V((INNER, INNER), BF16),
            V((3, KEYS, HEAD), BF16), V((3, KEYS, HEAD), BF16), V((3, 4 * TOK, HEAD), BF16),
            V((4, TOK, SHARD), BF16), V((4 * TOK, SHARD), BF16),
            V((12, 6, TOK, TOK), BF16), V((6, TOK, TOK), F32), V((12, 8, TOK), F32),
            V((3, 4 * TOK, HEAD), BF16), V((3, 4 * TOK, HEAD), BF16), V((TOK, INNER), BF16),
            V((3, 7 * TOK, HEAD), F32), V((3, 7 * TOK, HEAD), F32),
            V((3, HALO, HEAD), BF16), V((3, HALO, HEAD), BF16), V((3, HALO, HEAD), BF16), V((3, HALO, HEAD), BF16),
            V((3, 4 * TOK, HEAD), BF16), V((3, 4 * TOK, HEAD), BF16),
            V((3, HALO, HEAD), BF16), V((3, HALO, HEAD), BF16),
            V((3, 2, HEAD, INNER), F32), V((3, 2, HEAD, INNER), BF16), V((3, 2, HEAD, INNER), BF16),
            V((3, HEAD, INNER), BF16), V((3, HEAD, INNER), BF16), V((SHARD, INNER), F32),
            V((2, 96, INNER), BF16), V((2, 96, INNER), BF16), V((192, INNER), F32),
            V((8, 24, INNER), BF16), V((8, 24, INNER), BF16), V((4, 6, INNER), F32), V((3, 6, INNER), F32),
            dma((32,)), dma((3, 3, 3)), dma((3, 3, 3)), dma((4,)), dma((4,)), dma((4,)), dma((4,)),
            dma((2, 3)), dma((2, 3)),
            dma((3,)), dma((3,)), dma((3,)), dma((3,)),
            dma((3, 4)), dma((3, 4)), dma((3, 4)), dma((3, 4)), dma((2, 3, 3)), dma((2, 3, 3)),
            dma((2, 3)), dma((2, 3)),
            dma((3,)), dma((3,)), dma((3, 2)), dma((3, 2)), dma((2,)), dma((2,)), dma((8,)), dma((8,)), dma((3,)), dma((3,)),
        ],
        compiler_params=pltpu.CompilerParams(
            collective_id=0, has_side_effects=True, vmem_limit_bytes=62 * 1024 * 1024
        ),
    )(image_query[0], image_key[0], image_value[0], text_key[0], text_value[0], out_weight, cotangent[0])
    return img[None], dq[None], dk[None], dv[None], gw


def solution(mesh):
    part = P("fsdp", "seq", None)
    text = P("fsdp", None, None)
    return jax.shard_map(
        per_device, mesh=mesh,
        in_specs=(part, part, part, text, text, P("fsdp", None), part),
        out_specs=(part, part, part, part, P(("fsdp", "seq"), None)),
        check_vma=False,
    )
```
